32 devices in a mesh: lon: 8 (over z, x), lat: 4 (over y, core).
Axes of the slice: x: 2, y: 2, z: 4, core: 2. Of those that a mesh axis runs over, the one named last changes fastest.
Arguments:
- ocean_state: float32 [512, 4, 2, 1024], P('lat', None, None, 'lon'), may hold values from -4 to 4
- cotangent: float32 [512, 4, 2, 1024], P('lat', None, None, 'lon'), may hold values from -6 to 6
- features: bfloat16 [512, 64, 1024], P('lat', None, 'lon'), may hold values from -6 to 6
- w_in: bfloat16 [64, 256], replicated, may hold values from -0.75 to 0.75
- bias_in: float32 [256], replicated, may hold values from -3 to 3
- w_mid: bfloat16 [1, 256, 256], replicated, may hold values from -0.375 to 0.375
- w_out: bfloat16 [256, 2], replicated, may hold values from -0.375 to 0.375
- bias_out: float32 [2], replicated, may hold values from -3 to 3
- land_mask: int32 [512, 1024], P('lat', 'lon'), may hold values from 0 to 1, as said below
- home_slot: int32 [512, 8], P('lat', 'lon'), may hold values from -1 to 127, as said below
- owner_list: int32 [128, 8], P('lat', 'lon'), may hold values from 0 to 127, as said below
Outputs:
- new_state: float32 [512, 4, 2, 1024], P('lat', None, None, 'lon')
- state_adjoint: float32 [512, 4, 2, 1024], P('lat', None, None, 'lon')
- grad_w_in: float32 [64, 256], replicated
- grad_bias_in: float32 [256], replicated
- grad_w_mid: float32 [1, 256, 256], replicated
- grad_w_out: float32 [256, 2], replicated
- grad_bias_out: float32 [2], replicated
The draws below stay inside these ranges and needn't reach their ends.
Inputs may be any that keep to these rules, and one draw needn't show every extreme that they name: `land_mask`: A block is the 128 columns of one latitude row on one index of lon. Exactly half of the blocks of each latitude band hold a sea column; blocks without sea are all land; in every band some index of lon has sea in all its blocks. `home_slot`: -1 for a block without sea; else o * 16 + c: the block is the c-th that its device sends to owner o (the device of lon index o in the same band); a device uses the slots of one owner from c = 0 up. Every owner is sent exactly 64 blocks of its band, and in every band some device fills all its slots. `owner_list`: row b * 32 + r, column o: the r-th block that owner o of band b processes, as s * 16 + c, the block of lon index s whose home_slot is o * 16 + c. The entries of one owner are distinct; every owner lists exactly 32 of the blocks sent to it, and a sea block that its owner does not list is not processed.
All inputs are finite; a program needn't handle non-finite values.
Results may differ from the reference program's by a relative error of at most 0.0063.
The reference program's roundings to bfloat16 on the way count: a program that leaves them out, or rounds other values in their place, can miss the bound.
Values may be sent and summed in bfloat16 or wider, within the bound.
A program may use at most 64 MiB of HBM per device.

```python
import math
import jax
import jax.numpy as jnp
from jax import lax

LEV = 2
F_IN = 64
HID = 256
MIDS = 1
CLAT = 128
CLON = 128
CAP = 16
RECV = 32
LAT = 512
LON = 1024
N_LON = 8
N_LAT = 4


def band_plan(key):
    folded = jax.random.fold_in(key, 5)
    subkeys = jax.random.split(folded, 5)
    block_total = N_LON * CLAT
    wet_total = CLAT * N_LON // 2
    sent_each = CLAT // 2
    levels_drawn = jax.random.randint(subkeys[0], (N_LAT, N_LON), 0, 4)
    chosen = jax.random.randint(subkeys[1], (N_LAT, 1), 0, N_LON)
    device_ids = jnp.arange(N_LON, dtype=jnp.int32)[None, :]
    levels_drawn = jnp.where(device_ids == chosen, 4, levels_drawn)
    jitter = jax.random.randint(subkeys[2], (N_LAT, N_LON, CLAT), 0, 4096)
    scores = (levels_drawn[:, :, None] * 4096 + jitter).reshape(N_LAT, block_total) * block_total
    scores = scores + jnp.arange(block_total, dtype=jnp.int32)[None, :]
    ordering = jnp.argsort(-scores, axis=1)
    ranking = jnp.argsort(ordering, axis=1)
    wet_flag = (ranking < wet_total).astype(jnp.int32)
    running = jnp.cumsum(wet_flag, axis=1) - wet_flag
    per_device = wet_flag.reshape(N_LAT, N_LON, CLAT)
    device_count = jnp.sum(per_device, axis=2)
    device_start = jnp.cumsum(device_count, axis=1) - device_count
    order_index = running.reshape(N_LAT, N_LON, CLAT)
    owner_of = order_index % N_LON
    slot_of = (order_index - device_start[:, :, None]) // N_LON
    home_values = jnp.where(per_device > 0, owner_of * CAP + slot_of, -1)
    entry_values = device_ids[:, :, None] * CAP + slot_of
    arrival = order_index // N_LON
    keep_scores = jax.random.randint(subkeys[3], (N_LAT, N_LON, sent_each), 0, 4096) * sent_each
    keep_scores = keep_scores + jnp.arange(sent_each, dtype=jnp.int32)[None, None, :]
    keep_order = jnp.argsort(keep_scores, axis=2)
    keep_rank = jnp.argsort(keep_order, axis=2).astype(jnp.int32)
    keep_flat = keep_rank.reshape(N_LAT, N_LON * sent_each)
    lookup = jnp.minimum(owner_of * sent_each + arrival, N_LON * sent_each - 1).reshape(N_LAT, block_total)
    kept_rank = jnp.take_along_axis(keep_flat, lookup, axis=1).reshape(N_LAT, N_LON, CLAT)
    listed_flag = (per_device > 0) & (kept_rank < RECV)
    position = jnp.where(listed_flag, kept_rank, RECV)
    band_ids = jnp.broadcast_to(jnp.arange(N_LAT, dtype=jnp.int32)[:, None, None], position.shape)
    listed = jnp.zeros((N_LAT, RECV, N_LON), jnp.int32).at[band_ids, position, owner_of].set(entry_values, mode='drop')
    return (per_device, home_values, listed, subkeys[4])


def draw_land_mask(key, part):
    per_device, home_values, listed, extra_key = band_plan(key)
    block_wet = jnp.transpose(per_device, (0, 2, 1)).reshape(LAT, N_LON)
    column_wet = jnp.repeat(block_wet, CLON, axis=1)
    coastal = jax.random.randint(extra_key, (LAT, LON), 0, 5)
    first_column = (jnp.arange(LON, dtype=jnp.int32) % CLON == 0)[None, :]
    return (column_wet * ((coastal != 0) | first_column).astype(jnp.int32)).astype(jnp.int32)


def draw_home_slot(key, part):
    per_device, home_values, listed, extra_key = band_plan(key)
    return jnp.transpose(home_values, (0, 2, 1)).reshape(LAT, N_LON).astype(jnp.int32)


def draw_owner_list(key, part):
    per_device, home_values, listed, extra_key = band_plan(key)
    return listed.reshape(N_LAT * RECV, N_LON).astype(jnp.int32)


def steps_of(key, shape, pieces, low, high):
    def one(axis_at, shards_of):
        draws = jax.random.uniform(jax.random.fold_in(jax.random.fold_in(key, 6), axis_at), (shards_of,), jnp.float32, low / len(pieces), high / len(pieces))
        return jnp.repeat(jnp.exp(draws), shape[axis_at] // shards_of).reshape((-1,) + (1,) * (len(shape) - axis_at - 1))

    level = one(*pieces[0])
    for cut in pieces[1:]:
        level = level * one(*cut)
    return level


def gaussian(key, dims, spread, bound, pieces=(), held_as=jnp.bfloat16):
    loudness = steps_of(key, dims, pieces, -0.22, 0.18) if pieces else 1.0
    entries = jax.random.normal(key, dims, jnp.float32) * spread * loudness
    return jnp.minimum(jnp.maximum(entries, -bound), bound).astype(held_as)


def setup_inputs(seed: int = 0) -> dict:
    seeds = jax.random.split(jax.random.key(seed), 12)
    return {
        "ocean_state": gaussian(seeds[0], (LAT, 4, LEV, LON), 0.5, 4.0, ((0, 4), (3, 8)), jnp.float32),
        "cotangent": gaussian(seeds[1], (LAT, 4, LEV, LON), 1.0, 6.0, ((0, 4), (3, 8)), jnp.float32),
        "features": gaussian(seeds[2], (LAT, F_IN, LON), 1.0, 6.0, ((0, 4), (2, 8))),
        "w_in": gaussian(seeds[3], (F_IN, HID), F_IN ** -0.5, 0.75),
        "bias_in": gaussian(seeds[4], (HID,), 0.5, 3.0, (), jnp.float32),
        "w_mid": gaussian(seeds[5], (MIDS, HID, HID), HID ** -0.5, 0.375),
        "w_out": gaussian(seeds[6], (HID, LEV), HID ** -0.5, 0.375),
        "bias_out": gaussian(seeds[7], (LEV,), 1.0, 3.0, (), jnp.float32),
        "land_mask": draw_land_mask(jax.random.fold_in(seeds[11], 71), 0),
        "home_slot": draw_home_slot(jax.random.fold_in(seeds[11], 71), 0),
        "owner_list": draw_owner_list(jax.random.fold_in(seeds[11], 71), 0),
    }


kappa_most = 0.2

def local_update(state_pad, kappa_pad, sea_pad):
    east_open = (sea_pad[1:-1, :-1] * sea_pad[1:-1, 1:])[:, None, :]
    east_speed = 0.5 * (state_pad[1:-1, 2, :, :-1] + state_pad[1:-1, 2, :, 1:]) * east_open
    east_kappa = 0.5 * (kappa_pad[1:-1, :, :-1] + kappa_pad[1:-1, :, 1:]) * east_open
    west_side = state_pad[1:-1, :, :, :-1]
    east_side = state_pad[1:-1, :, :, 1:]
    east_flux = east_speed[:, None] * 0.5 * (west_side + east_side) - east_kappa[:, None] * (east_side - west_side)
    north_open = (sea_pad[:-1, 1:-1] * sea_pad[1:, 1:-1])[:, None, :]
    north_speed = 0.5 * (state_pad[:-1, 3, :, 1:-1] + state_pad[1:, 3, :, 1:-1]) * north_open
    north_kappa = 0.5 * (kappa_pad[:-1, :, 1:-1] + kappa_pad[1:, :, 1:-1]) * north_open
    south_side = state_pad[:-1, :, :, 1:-1]
    north_side = state_pad[1:, :, :, 1:-1]
    north_flux = north_speed[:, None] * 0.5 * (south_side + north_side) - north_kappa[:, None] * (north_side - south_side)
    centre = state_pad[1:-1, :, :, 1:-1]
    return centre - (east_flux[..., 1:] - east_flux[..., :-1]) - (north_flux[1:] - north_flux[:-1])

def wrap_lon(values):
    return jnp.concatenate([values[..., -1:], values, values[..., :1]], axis=-1)

def closure_cells(cell_features, w_in, bias_in, w_mid, w_out, bias_out):
    first = jnp.dot(w_in.T, cell_features, preferred_element_type=jnp.float32) + bias_in[:, None]
    hidden = jnp.tanh(first).astype(jnp.bfloat16)
    layers = [hidden]
    for layer_index in range(MIDS):
        hidden = jnp.tanh(jnp.dot(w_mid[layer_index].T, hidden, preferred_element_type=jnp.float32)).astype(jnp.bfloat16)
        layers.append(hidden)
    logits = jnp.dot(w_out.T, hidden, preferred_element_type=jnp.float32) + bias_out[:, None]
    return (layers, jax.nn.sigmoid(logits))

def reference(ocean_state, cotangent, features, w_in, bias_in, w_mid, w_out, bias_out, land_mask, home_slot, owner_list):
    band_home = home_slot.reshape(N_LAT, CLAT, N_LON)
    shape_home = band_home.shape
    band_ids = jnp.broadcast_to(jnp.arange(N_LAT, dtype=jnp.int32)[:, None, None], shape_home)
    row_ids = jnp.broadcast_to(jnp.arange(CLAT, dtype=jnp.int32)[None, :, None], shape_home)
    device_ids = jnp.broadcast_to(jnp.arange(N_LON, dtype=jnp.int32)[None, None, :], shape_home)
    slot_spot = jnp.where(band_home >= 0, band_home, N_LON * CAP).astype(jnp.int32)
    slot_row = jnp.zeros((N_LAT, N_LON, N_LON * CAP), jnp.int32).at[band_ids, device_ids, slot_spot].set(row_ids, mode='drop')
    listed = owner_list.reshape(N_LAT, RECV, N_LON)
    shape_list = listed.shape
    list_band = jnp.broadcast_to(jnp.arange(N_LAT, dtype=jnp.int32)[:, None, None], shape_list)
    owner_ids = jnp.broadcast_to(jnp.arange(N_LON, dtype=jnp.int32)[None, None, :], shape_list)
    source = (listed // CAP).astype(jnp.int32)
    wanted = (owner_ids * CAP + listed % CAP).astype(jnp.int32)
    block_row = (slot_row[list_band, source, wanted] + list_band * CLAT).astype(jnp.int32)
    block_rows = block_row.reshape(N_LAT * RECV, N_LON)
    block_devs = source.reshape(N_LAT * RECV, N_LON)
    features_split = features.reshape(LAT, F_IN, N_LON, CLON)

    def gather_cells(group_rows, group_devs):
        picked = features_split[group_rows, :, group_devs, :]
        return picked.transpose(1, 0, 2).reshape(F_IN, N_LON * CLON)

    def forward_group(indices):
        group_rows, group_devs = indices
        layers, squashed = closure_cells(gather_cells(group_rows, group_devs), w_in, bias_in, w_mid, w_out, bias_out)
        return (kappa_most * squashed).reshape(LEV, N_LON, CLON).transpose(1, 0, 2)
    group_kappa = lax.map(forward_group, (block_rows, block_devs))
    kappa_blocks = jnp.zeros((LAT, N_LON, LEV, CLON), jnp.float32).at[block_rows, block_devs].set(group_kappa)
    diffusivity = kappa_blocks.transpose(0, 2, 1, 3).reshape(LAT, LEV, LON)
    sea = land_mask.astype(jnp.float32)
    sea_pad = jnp.pad(wrap_lon(sea), ((1, 1), (0, 0)))

    def stepper(state_in, kappa_in):
        state_pad = jnp.pad(wrap_lon(state_in), ((1, 1), (0, 0), (0, 0), (0, 0)))
        kappa_pad = jnp.pad(wrap_lon(kappa_in), ((1, 1), (0, 0), (0, 0)))
        return local_update(state_pad, kappa_pad, sea_pad)
    new_state, pullback = jax.vjp(stepper, ocean_state, diffusivity)
    state_adjoint, kappa_grad = pullback(cotangent)
    kappa_low = kappa_grad.astype(jnp.bfloat16)
    kappa_split = kappa_low.reshape(LAT, LEV, N_LON, CLON)

    def backward_group(running, indices):
        group_rows, group_devs = indices
        cells = gather_cells(group_rows, group_devs)
        layers, squashed = closure_cells(cells, w_in, bias_in, w_mid, w_out, bias_out)
        grad_cells = kappa_split[group_rows, :, group_devs, :].transpose(1, 0, 2).reshape(LEV, N_LON * CLON)
        logit_grad = grad_cells.astype(jnp.float32) * (kappa_most * squashed * (1.0 - squashed))
        logit_low = logit_grad.astype(jnp.bfloat16)
        sum_out = jnp.dot(layers[-1], logit_low.T, preferred_element_type=jnp.float32)
        sum_bias_out = lax.optimization_barrier(jnp.sum(logit_grad, axis=1))
        carried = jnp.dot(w_out, logit_low, preferred_element_type=jnp.float32)
        mid_sums = []
        for layer_index in range(MIDS, 0, -1):
            current = layers[layer_index].astype(jnp.float32)
            layer_grad = (carried * (1.0 - current * current)).astype(jnp.bfloat16)
            mid_sums.insert(0, jnp.dot(layers[layer_index - 1], layer_grad.T, preferred_element_type=jnp.float32))
            carried = jnp.dot(w_mid[layer_index - 1], layer_grad, preferred_element_type=jnp.float32)
        base_float = layers[0].astype(jnp.float32)
        first_grad = carried * (1.0 - base_float * base_float)
        sum_bias_in = lax.optimization_barrier(jnp.sum(first_grad, axis=1))
        sum_in = jnp.dot(cells, first_grad.astype(jnp.bfloat16).T, preferred_element_type=jnp.float32)
        summed = (running[0] + sum_in, running[1] + sum_bias_in, running[2] + jnp.stack(mid_sums), running[3] + sum_out, running[4] + sum_bias_out)
        return (summed, None)
    initial = (jnp.zeros((F_IN, HID), jnp.float32), jnp.zeros((HID,), jnp.float32), jnp.zeros((MIDS, HID, HID), jnp.float32), jnp.zeros((HID, LEV), jnp.float32), jnp.zeros((LEV,), jnp.float32))
    totals, unused = lax.scan(backward_group, initial, (block_rows, block_devs))
    scaling = 1.0 / math.sqrt(CLAT * CLON)
    return (new_state, state_adjoint, totals[0] * scaling, totals[1] * scaling, totals[2] * scaling, totals[3] * scaling, totals[4] * scaling)
```

```python
import functools
import math

import jax
import jax.numpy as jnp
from jax import lax
from jax.experimental import pallas as pl
from jax.experimental.pallas import tpu as pltpu
from jax.sharding import PartitionSpec as P

kappa_most = 0.2
GROUP = 4
CHUNK = 16
F32 = jnp.float32
BF16 = jnp.bfloat16
EXACT = lax.Precision.HIGHEST
NT = (((1,), (1,)), ((), ()))
TN = (((0,), (0,)), ((), ()))


def lane_of(shape):
    return lax.broadcasted_iota(jnp.int32, shape, len(shape) - 1)


def edge_picker(width):
    rows = lax.broadcasted_iota(jnp.int32, (8, width), 0)
    lanes = lax.broadcasted_iota(jnp.int32, (8, width), 1)
    hit = ((rows == 0) & (lanes == 0)) | ((rows == 1) & (lanes == width - 1))
    return hit.astype(F32)


def spread_edges(halo, width):
    return lax.dot_general(
        halo, edge_picker(width), TN, precision=EXACT, preferred_element_type=F32
    )


def pack_edges(values):
    return lax.dot_general(
        edge_picker(values.shape[1]), values, NT, precision=EXACT, preferred_element_type=F32
    )


def between(west, east):
    return jnp.concatenate([west[1:2], east[0:1], jnp.zeros((6, west.shape[1]), F32)], axis=0)


def ring(axis, step):
    count = lax.axis_size(axis)
    return lax.rem(lax.axis_index(axis) + (step + count), count)


def push(source, target, sems, index, axis, step):
    send, recv = sems
    copy = pltpu.make_async_remote_copy(
        src_ref=source,
        dst_ref=target,
        send_sem=send.at[index],
        recv_sem=recv.at[index],
        device_id={axis: ring(axis, step)},
        device_id_type=pl.DeviceIdType.MESH,
    )
    copy.start()
    return copy


def greet(peers):
    barrier = pltpu.get_barrier_semaphore()
    for axis, step in peers:
        pl.semaphore_signal(
            barrier,
            inc=1,
            device_id={axis: ring(axis, step)},
            device_id_type=pl.DeviceIdType.MESH,
        )
    pl.semaphore_wait(barrier, len(peers))


def halo_kernel(
    state_ref,
    cot_ref,
    sea_ref,
    home_ref,
    list_ref,
    flags_ref,
    state_edge_ref,
    cot_edge_ref,
    sea_edge_ref,
    state_rows_ref,
    cot_rows_ref,
    sea_rows_ref,
    lists,
    edge_out,
    edge_in,
    rows_out,
    rows_in,
    list_send,
    list_recv,
    halo_send,
    halo_recv,
):
    rows, subs, width = state_ref.shape
    span = rows * subs
    lon_count = lax.axis_size("lon")
    cap = rows // lon_count
    lat_index = lax.axis_index("lat")
    peers = [("lon", d) for d in range(1, lon_count)] + [("lat", 1), ("lat", -1)]
    greet(peers)
    copies = []
    for d in range(1, lon_count):
        copies.append(push(list_ref, lists.at[d], (list_send, list_recv), d, "lon", d))
    for side, row in ((0, 0), (1, rows - 1)):
        rows_out[side, 0:subs] = state_ref[row]
        rows_out[side, subs : 2 * subs] = cot_ref[row]
        rows_out[side, 2 * subs : 2 * subs + 8] = jnp.broadcast_to(
            sea_ref[row : row + 1], (8, width)
        )
    halo = (halo_send, halo_recv)
    copies.append(push(rows_out.at[0], rows_in.at[1], halo, 0, "lat", -1))
    copies.append(push(rows_out.at[1], rows_in.at[0], halo, 1, "lat", 1))
    edge_out[:, 0:span] = pack_edges(state_ref[...].reshape(span, width))
    edge_out[:, span : 2 * span] = pack_edges(cot_ref[...].reshape(span, width))
    edge_out[:, 2 * span :] = pack_edges(sea_ref[...])
    copies.append(push(edge_out, edge_in.at[1], halo, 2, "lon", -1))
    copies.append(push(edge_out, edge_in.at[0], halo, 3, "lon", 1))
    for copy in copies:
        copy.wait()

    me = lax.axis_index("lon")
    home = home_ref[...]
    found = jnp.zeros(list_ref.shape, jnp.int32)
    for d in range(lon_count):
        entries = list_ref[...] if d == 0 else lists[d]
        owner = ring("lon", -d)
        source = entries // cap
        wanted = owner * cap + (entries - source * cap)
        hit = (source == me) & (wanted == home)
        found = jnp.where(hit, 1, found)
    flags_ref[...] = jnp.max(found, axis=0, keepdims=True)
    edges = between(edge_in[0], edge_in[1])
    state_edge_ref[...] = edges[:, 0:span]
    cot_edge_ref[...] = edges[:, span : 2 * span]
    sea_edge_ref[...] = edges[:, 2 * span :]
    inside = (lat_index > 0, lat_index < lax.axis_size("lat") - 1)
    state_rows_ref[...] = rows_in[:, 0:subs]
    cot_rows_ref[...] = rows_in[:, subs : 2 * subs]
    for side in range(2):
        open_here = jnp.where(inside[side], 1.0, 0.0)
        sea_rows_ref[side : side + 1] = rows_in[side, 2 * subs : 2 * subs + 1] * open_here
    sea_rows_ref[2:8] = jnp.zeros((6, width), F32)


def west_of(values, edge):
    rolled = pltpu.roll(values, 1, values.ndim - 1)
    return jnp.where(lane_of(values.shape) == 0, edge, rolled)


def east_of(values, edge):
    width = values.shape[-1]
    rolled = pltpu.roll(values, width - 1, values.ndim - 1)
    return jnp.where(lane_of(values.shape) == width - 1, edge, rolled)


def field_sum(values):
    values = values + pltpu.roll(values, 2, 1)
    return values + pltpu.roll(values, 4, 1)


def repeat_field(values, field):
    sub = lax.broadcasted_iota(jnp.int32, values.shape, 1)
    picked = jnp.where(sub // 2 == field, values, 0.0)
    return field_sum(picked)


def padded_load(ref, edges, start, size, total, offset):
    middle = ref[pl.ds(start, size)]
    if offset < 0:
        below = ref[pl.ds(jnp.maximum(start - 1, 0), 1)]
        below = jnp.where(start == 0, edges[0:1], below)
        return jnp.concatenate([below, middle[:-1]], axis=0)
    above = ref[pl.ds(jnp.minimum(start + size, total - 1), 1)]
    above = jnp.where(start + size >= total, edges[1:2], above)
    return jnp.concatenate([middle[1:], above], axis=0)


def prepare_sea(sea_ref, sea_edge_ref, sea_rows_ref, open_refs):
    rows, width = sea_ref.shape
    sea = sea_ref[...]
    edge = spread_edges(sea_edge_ref[...], width)
    south = jnp.concatenate([sea_rows_ref[0:1], sea[:-1]], axis=0)
    north = jnp.concatenate([sea[1:], sea_rows_ref[1:2]], axis=0)
    for ref, other in zip(open_refs, (west_of(sea, edge), east_of(sea, edge), south, north)):
        ref[...] = sea * other


def closure_kernel(
    flags_ref,
    features_ref,
    state_ref,
    cot_ref,
    sea_ref,
    state_edge_ref,
    cot_edge_ref,
    sea_edge_ref,
    state_rows_ref,
    cot_rows_ref,
    sea_rows_ref,
    w_in_ref,
    w_mid_ref,
    small_ref,
    bias_out_ref,
    diff_ref,
    diff_edge_ref,
    sums_ref,
    open_w,
    open_e,
    open_s,
    open_n,
    state_x,
    cot_x,
    kgrad,
    w_in_t,
    w_mid_t,
    bias_in_col,
    w_out_rep,
    w_out_col,
    acc_in,
    acc_mid,
    acc_out,
    acc_bias,
    acc_bout,
    order,
):
    rows, subs, width = state_ref.shape
    hid = w_mid_ref.shape[0]

    def note(row, count):
        order[count] = row
        return count + flags_ref[row]

    count = lax.fori_loop(0, rows, note, jnp.int32(0))
    for extra in range(GROUP):
        order[count + extra] = rows

    prepare_sea(sea_ref, sea_edge_ref, sea_rows_ref, (open_w, open_e, open_s, open_n))
    state_x[...] = spread_edges(state_edge_ref[...], width).reshape(rows, subs, width)
    cot_x[...] = spread_edges(cot_edge_ref[...], width).reshape(rows, subs, width)

    def kappa_chunk(step, carry):
        start = pl.multiple_of(step * CHUNK, CHUNK)
        at = pl.ds(start, CHUNK)
        q = state_ref[at]
        g = cot_ref[at]
        qx = state_x[at]
        gx = cot_x[at]

        def part(opened, q_near, g_near):
            return (g_near - g) * (q_near - q) * opened[at][:, None, :]

        total = part(open_w, west_of(q, qx), west_of(g, gx))
        total += part(open_e, east_of(q, qx), east_of(g, gx))
        total += part(
            open_s,
            padded_load(state_ref, state_rows_ref, start, CHUNK, rows, -1),
            padded_load(cot_ref, cot_rows_ref, start, CHUNK, rows, -1),
        )
        total += part(
            open_n,
            padded_load(state_ref, state_rows_ref, start, CHUNK, rows, 1),
            padded_load(cot_ref, cot_rows_ref, start, CHUNK, rows, 1),
        )
        kgrad[at] = field_sum(total) * -0.5
        diff_ref[at] = jnp.zeros((CHUNK, subs, width), F32)
        return carry

    lax.fori_loop(0, rows // CHUNK, kappa_chunk, 0)
    kgrad[pl.ds(rows, 8)] = jnp.zeros((8, subs, width), F32)

    small_t = small_ref[...].T
    bias_in_col[...] = jnp.broadcast_to(small_t[:, 8:9], (hid, width))
    w_out_rep[...] = small_ref[0:8].astype(BF16)
    w_out_col[...] = jnp.where(lane_of((hid, 8)) < 2, small_t[:, 0:8], 0.0).astype(BF16)
    w_in_t[...] = w_in_ref[...].astype(F32).T.astype(BF16)
    w_mid_t[...] = w_mid_ref[...].astype(F32).T.astype(BF16)
    for ref in (acc_in, acc_mid, acc_out, acc_bias, acc_bout):
        ref[...] = jnp.zeros(ref.shape, F32)

    def group(step, carry):
        picked = [order[step * GROUP + i] for i in range(GROUP)]
        loads = [jnp.minimum(row, rows - 1) for row in picked]
        x = jnp.concatenate([features_ref[row] for row in loads], axis=1)
        kap = jnp.concatenate([kgrad[row] for row in picked], axis=1)
        bias_in = jnp.concatenate([bias_in_col[...]] * GROUP, axis=1)
        first = jnp.dot(w_in_t[...], x, preferred_element_type=F32) + bias_in
        h0 = jnp.tanh(first).astype(BF16)
        h1 = jnp.tanh(jnp.dot(w_mid_t[...], h0, preferred_element_type=F32)).astype(BF16)
        logits = jnp.dot(w_out_rep[...], h1, preferred_element_type=F32)
        logits = logits + jnp.concatenate([bias_out_ref[...]] * GROUP, axis=1)
        squashed = 1.0 / (1.0 + jnp.exp(-logits))
        for i, row in enumerate(picked):
            diff_ref[row] = kappa_most * squashed[:, i * width : (i + 1) * width]
        kap_low = kap.astype(BF16).astype(F32)
        logit_grad = kap_low * (kappa_most * squashed * (1.0 - squashed))
        logit_low = logit_grad.astype(BF16)
        acc_out[...] += lax.dot_general(logit_low, h1, NT, preferred_element_type=F32)
        acc_bout[...] += functools.reduce(
            jnp.add, [logit_grad[:, i * width : (i + 1) * width] for i in range(GROUP)]
        )
        carried = jnp.dot(w_out_col[...], logit_low, preferred_element_type=F32)
        current = h1.astype(F32)
        layer_grad = (carried * (1.0 - current * current)).astype(BF16)
        acc_mid[...] += lax.dot_general(h0, layer_grad, NT, preferred_element_type=F32)
        carried = jnp.dot(w_mid_ref[...], layer_grad, preferred_element_type=F32)
        base = h0.astype(F32)
        first_grad = carried * (1.0 - base * base)
        acc_bias[...] += functools.reduce(
            jnp.add, [first_grad[:, i * width : (i + 1) * width] for i in range(GROUP)]
        )
        acc_in[...] += lax.dot_general(
            x, first_grad.astype(BF16), NT, preferred_element_type=F32
        )
        return carry

    lax.fori_loop(0, (count + GROUP - 1) // GROUP, group, 0)

    scaling = 1.0 / math.sqrt(rows * width)
    f_in = w_in_ref.shape[0]
    ones = jnp.ones((8, width), F32)
    row_bias = lax.dot_general(ones, acc_bias[...], NT, precision=EXACT, preferred_element_type=F32)
    tall = jnp.concatenate([acc_bout[...], jnp.zeros((hid - 8, width), F32)], axis=0)
    row_bout = lax.dot_general(ones, tall, NT, precision=EXACT, preferred_element_type=F32)
    which = lax.broadcasted_iota(jnp.int32, (8, hid), 0)
    misc = jnp.where(which < 2, acc_out[...], jnp.where(which == 2, row_bias, row_bout))
    misc = jnp.where(which < 4, misc, 0.0)
    diff_edge_ref[...] = pack_edges(diff_ref[0:rows].reshape(rows * subs, width))
    tiles = 0
    for block in (acc_mid[...], acc_in[...], misc):
        for half in range(hid // width):
            count = block.shape[0] // 8
            part = block[:, half * width : (half + 1) * width] * scaling
            sums_ref[tiles : tiles + count] = part.reshape(count, 8, width)
            tiles += count
    spare = sums_ref.shape[0] - tiles
    if spare:
        sums_ref[tiles : tiles + spare] = jnp.zeros((spare, 8, width), F32)


def stencil_kernel(
    state_ref,
    cot_ref,
    sea_ref,
    diff_ref,
    state_edge_ref,
    cot_edge_ref,
    sea_edge_ref,
    diff_edge_ref,
    state_rows_ref,
    cot_rows_ref,
    sea_rows_ref,
    sums_ref,
    new_ref,
    adj_ref,
    grad_in_ref,
    grad_bias_in_ref,
    grad_mid_ref,
    grad_out_ref,
    grad_bias_out_ref,
    open_w,
    open_e,
    open_s,
    open_n,
    state_x,
    cot_x,
    diff_x,
    diff_rows_ref,
    edge_in,
    from_lat,
    for_lon,
    from_lon,
    chunk_sum,
    gathered,
    full,
    halo_send,
    halo_recv,
    lat_send,
    lat_recv,
    lon_send,
    lon_recv,
):
    rows, subs, width = state_ref.shape
    lat_count, lon_count = sums_ref.shape[:2]
    lat_me = lax.axis_index("lat")
    lon_me = lax.axis_index("lon")
    lat_steps = range(1, lat_count)
    lon_steps = range(1, lon_count)
    greet([("lon", d) for d in lon_steps] + [("lat", d) for d in lat_steps])
    halo = (halo_send, halo_recv)
    halo_copies = [
        push(diff_ref.at[0], diff_rows_ref.at[1], halo, 0, "lat", -1),
        push(diff_ref.at[rows - 1], diff_rows_ref.at[0], halo, 1, "lat", 1),
        push(diff_edge_ref, edge_in.at[1], halo, 2, "lon", -1),
        push(diff_edge_ref, edge_in.at[0], halo, 3, "lon", 1),
    ]
    lat_sems = (lat_send, lat_recv)
    lon_sems = (lon_send, lon_recv)
    reduce_lat = [
        push(sums_ref.at[ring("lat", d)], from_lat.at[d], lat_sems, d, "lat", d) for d in lat_steps
    ]
    prepare_sea(sea_ref, sea_edge_ref, sea_rows_ref, (open_w, open_e, open_s, open_n))
    state_x[...] = spread_edges(state_edge_ref[...], width).reshape(rows, subs, width)
    cot_x[...] = spread_edges(cot_edge_ref[...], width).reshape(rows, subs, width)
    for copy in halo_copies:
        copy.wait()
    diff_x[...] = spread_edges(between(edge_in[0], edge_in[1]), width).reshape(rows, subs, width)

    def chunk(step, carry):
        start = pl.multiple_of(step * CHUNK, CHUNK)
        at = pl.ds(start, CHUNK)
        q = state_ref[at]
        g = cot_ref[at]
        k = diff_ref[at]
        sub = lax.broadcasted_iota(jnp.int32, q.shape, 1)

        def face(sign, field, opened, q_near, g_near, k_near):
            gate = opened[at][:, None, :]
            speed = repeat_field(q + q_near, field) * (0.5 * gate)
            kf = (k + k_near) * (0.5 * gate)
            q_sum = 0.5 * (q + q_near)
            g_diff = g_near - g
            new_part = kf * (q_near - q) - sign * speed * q_sum
            w_part = field_sum(g_diff * q_sum) * ((0.5 * sign) * gate)
            adj_part = g_diff * (kf + (0.5 * sign) * speed)
            adj_part = adj_part + jnp.where(sub // 2 == field, w_part, 0.0)
            return new_part, adj_part

        qx, gx, kx = state_x[at], cot_x[at], diff_x[at]
        parts = [
            face(-1.0, 2, open_w, west_of(q, qx), west_of(g, gx), west_of(k, kx)),
            face(1.0, 2, open_e, east_of(q, qx), east_of(g, gx), east_of(k, kx)),
        ]
        for sign, offset, opened in ((-1.0, -1, open_s), (1.0, 1, open_n)):
            parts.append(
                face(
                    sign,
                    3,
                    opened,
                    padded_load(state_ref, state_rows_ref, start, CHUNK, rows, offset),
                    padded_load(cot_ref, cot_rows_ref, start, CHUNK, rows, offset),
                    padded_load(diff_ref, diff_rows_ref, start, CHUNK, rows, offset),
                )
            )
        new_ref[at] = q + parts[0][0] + parts[1][0] + parts[2][0] + parts[3][0]
        adj_ref[at] = g + parts[0][1] + parts[1][1] + parts[2][1] + parts[3][1]
        return carry

    steps = rows // CHUNK
    lax.fori_loop(0, steps // 2, chunk, 0)
    for copy in reduce_lat:
        copy.wait()
    total = sums_ref[lat_me]
    for d in lat_steps:
        total = total + from_lat[d]
    for_lon[...] = total
    reduce_lon = [
        push(for_lon.at[ring("lon", d)], from_lon.at[d], lon_sems, d, "lon", d) for d in lon_steps
    ]
    lax.fori_loop(steps // 2, steps, chunk, 0)
    for copy in reduce_lon:
        copy.wait()
    total = for_lon[lon_me]
    for d in lon_steps:
        total = total + from_lon[d]
    chunk_sum[...] = total
    gathered[lon_me] = total
    spread_lon = [
        push(chunk_sum, gathered.at[lon_me], lon_sems, lon_count + d, "lon", d) for d in lon_steps
    ]
    for copy in spread_lon:
        copy.wait()
    spread_lat = [
        push(gathered, full.at[lat_me], lat_sems, lat_count + d, "lat", d) for d in lat_steps
    ]
    full[lat_me] = gathered[...]
    for copy in spread_lat:
        copy.wait()

    hid = grad_mid_ref.shape[0]
    flat = full[...].reshape(lat_count * lon_count * full.shape[2], 8, width)
    tiles = 0
    halves = hid // width
    for ref in (grad_mid_ref, grad_in_ref):
        count = ref.shape[0] // 8
        for half in range(halves):
            ref[:, half * width : (half + 1) * width] = flat[tiles : tiles + count].reshape(
                8 * count, width
            )
            tiles += count
    misc = jnp.concatenate([flat[tiles + half] for half in range(halves)], axis=1)
    levels = grad_out_ref.shape[1]
    grad_bias_in_ref[...] = misc[2:3]
    grad_bias_out_ref[...] = misc[3:4, 0:levels]
    grad_out_ref[...] = misc.T[:, 0:levels]


def on_device(
    ocean_state,
    cotangent,
    features,
    w_in,
    bias_in,
    w_mid,
    w_out,
    bias_out,
    land_mask,
    home_slot,
    owner_list,
):
    rows, fields, levels, width = ocean_state.shape
    subs = fields * levels
    f_in, hid = w_in.shape
    lon_count = lax.axis_size("lon")
    lat_count = lax.axis_size("lat")

    state = ocean_state.reshape(rows, subs, width)
    cot = cotangent.reshape(rows, subs, width)
    sea = land_mask.astype(F32)
    span = rows * subs
    vmem = pl.BlockSpec(memory_space=pltpu.VMEM)
    smem = pl.BlockSpec(memory_space=pltpu.SMEM)
    dma = pltpu.SemaphoreType.DMA
    listed = owner_list.shape[0]
    flags, state_edge, cot_edge, sea_edge, state_rows, cot_rows, sea_rows = pl.pallas_call(
        halo_kernel,
        name="halo",
        out_shape=(
            jax.ShapeDtypeStruct((1, rows), jnp.int32),
            jax.ShapeDtypeStruct((8, span), F32),
            jax.ShapeDtypeStruct((8, span), F32),
            jax.ShapeDtypeStruct((8, rows), F32),
            jax.ShapeDtypeStruct((2, subs, width), F32),
            jax.ShapeDtypeStruct((2, subs, width), F32),
            jax.ShapeDtypeStruct((8, width), F32),
        ),
        in_specs=[vmem] * 5,
        out_specs=(vmem,) * 7,
        scratch_shapes=[
            pltpu.VMEM((lon_count, listed, rows), jnp.int32),
            pltpu.VMEM((8, 2 * span + rows), F32),
            pltpu.VMEM((2, 8, 2 * span + rows), F32),
            pltpu.VMEM((2, 2 * subs + 8, width), F32),
            pltpu.VMEM((2, 2 * subs + 8, width), F32),
            dma((lon_count,)),
            dma((lon_count,)),
            dma((4,)),
            dma((4,)),
        ],
        compiler_params=pltpu.CompilerParams(
            collective_id=0, has_side_effects=True, vmem_limit_bytes=32 * 1024 * 1024
        ),
    )(
        state,
        cot,
        sea,
        home_slot.reshape(1, rows),
        jnp.broadcast_to(owner_list, (listed, rows)),
    )
    flags = flags.reshape(rows)

    small = jnp.concatenate(
        [
            jnp.tile(w_out.astype(F32).T, (8 // levels, 1)),
            bias_in[None],
            jnp.zeros((7, hid), F32),
        ],
        axis=0,
    )
    bias_out_rep = jnp.broadcast_to(jnp.tile(bias_out, (8 // levels,))[:, None], (8, width))

    tiles = (hid // width) * (hid + f_in + 8) // 8
    share = -(-tiles // (lat_count * lon_count))
    mask = pltpu.VMEM((rows, width), F32)
    slab = pltpu.VMEM((rows, subs, width), F32)
    diff, diff_edge, sums = pl.pallas_call(
        closure_kernel,
        name="closure",
        out_shape=(
            jax.ShapeDtypeStruct((rows + 8, subs, width), F32),
            jax.ShapeDtypeStruct((8, span), F32),
            jax.ShapeDtypeStruct((lat_count * lon_count * share, 8, width), F32),
        ),
        in_specs=[smem] + [vmem] * 14,
        out_specs=(vmem,) * 3,
        scratch_shapes=[
            mask,
            mask,
            mask,
            mask,
            slab,
            slab,
            pltpu.VMEM((rows + 8, subs, width), F32),
            pltpu.VMEM((hid, f_in), BF16),
            pltpu.VMEM((hid, hid), BF16),
            pltpu.VMEM((hid, width), F32),
            pltpu.VMEM((8, hid), BF16),
            pltpu.VMEM((hid, 8), BF16),
            pltpu.VMEM((f_in, hid), F32),
            pltpu.VMEM((hid, hid), F32),
            pltpu.VMEM((8, hid), F32),
            pltpu.VMEM((hid, width), F32),
            pltpu.VMEM((8, width), F32),
            pltpu.SMEM((rows + 2 * GROUP,), jnp.int32),
        ],
        compiler_params=pltpu.CompilerParams(vmem_limit_bytes=40 * 1024 * 1024),
    )(
        flags,
        features,
        state,
        cot,
        sea,
        state_edge,
        cot_edge,
        sea_edge,
        state_rows,
        cot_rows,
        sea_rows,
        w_in,
        w_mid[0],
        small,
        bias_out_rep,
    )

    piece = (share, 8, width)
    new_state, adjoint, grad_in, grad_bias_in, grad_mid, grad_out, grad_bias_out = pl.pallas_call(
        stencil_kernel,
        name="stencil",
        out_shape=(
            jax.ShapeDtypeStruct((rows, subs, width), F32),
            jax.ShapeDtypeStruct((rows, subs, width), F32),
            jax.ShapeDtypeStruct((f_in, hid), F32),
            jax.ShapeDtypeStruct((1, hid), F32),
            jax.ShapeDtypeStruct((hid, hid), F32),
            jax.ShapeDtypeStruct((hid, levels), F32),
            jax.ShapeDtypeStruct((1, levels), F32),
        ),
        in_specs=[vmem] * 12,
        out_specs=(vmem,) * 7,
        scratch_shapes=[
            mask,
            mask,
            mask,
            mask,
            slab,
            slab,
            slab,
            pltpu.VMEM((2, subs, width), F32),
            pltpu.VMEM((2, 8, span), F32),
            pltpu.VMEM((lat_count, lon_count) + piece, F32),
            pltpu.VMEM((lon_count,) + piece, F32),
            pltpu.VMEM((lon_count,) + piece, F32),
            pltpu.VMEM(piece, F32),
            pltpu.VMEM((lon_count,) + piece, F32),
            pltpu.VMEM((lat_count, lon_count) + piece, F32),
            dma((4,)),
            dma((4,)),
            dma((2 * lat_count,)),
            dma((2 * lat_count,)),
            dma((2 * lon_count,)),
            dma((2 * lon_count,)),
        ],
        compiler_params=pltpu.CompilerParams(
            collective_id=1, has_side_effects=True, vmem_limit_bytes=32 * 1024 * 1024
        ),
    )(
        state,
        cot,
        sea,
        diff,
        state_edge,
        cot_edge,
        sea_edge,
        diff_edge,
        state_rows,
        cot_rows,
        sea_rows,
        sums.reshape((lat_count, lon_count) + piece),
    )
    return (
        new_state.reshape(ocean_state.shape),
        adjoint.reshape(ocean_state.shape),
        grad_in,
        grad_bias_in[0],
        grad_mid[None],
        grad_out,
        grad_bias_out[0],
    )


def solution(mesh):
    in_specs = (
        P("lat", None, None, "lon"),
        P("lat", None, None, "lon"),
        P("lat", None, "lon"),
        P(),
        P(),
        P(),
        P(),
        P(),
        P("lat", "lon"),
        P("lat", "lon"),
        P("lat", "lon"),
    )
    out_specs = (P("lat", None, None, "lon"), P("lat", None, None, "lon"), P(), P(), P(), P(), P())
    return jax.shard_map(
        on_device, mesh=mesh, in_specs=in_specs, out_specs=out_specs, check_vma=False
    )
```

```python
import functools
import math

import jax
import jax.numpy as jnp
from jax import lax
from jax.experimental import pallas as pl
from jax.experimental.pallas import tpu as pltpu
from jax.sharding import PartitionSpec as P

kappa_most = 0.2
GROUP = 8
CHUNK = 16
F32 = jnp.float32
BF16 = jnp.bfloat16
EXACT = lax.Precision.HIGHEST
NT = (((1,), (1,)), ((), ()))
TN = (((0,), (0,)), ((), ()))


def lane_of(shape):
    return lax.broadcasted_iota(jnp.int32, shape, len(shape) - 1)


def edge_picker(width):
    rows = lax.broadcasted_iota(jnp.int32, (8, width), 0)
    lanes = lax.broadcasted_iota(jnp.int32, (8, width), 1)
    hit = ((rows == 0) & (lanes == 0)) | ((rows == 1) & (lanes == width - 1))
    return hit.astype(F32)


def spread_edges(halo, width):
    return lax.dot_general(
        halo, edge_picker(width), TN, precision=EXACT, preferred_element_type=F32
    )


def pack_edges(values):
    return lax.dot_general(
        edge_picker(values.shape[1]), values, NT, precision=EXACT, preferred_element_type=F32
    )


def between(west, east):
    return jnp.concatenate([west[1:2], east[0:1], jnp.zeros((6, west.shape[1]), F32)], axis=0)


def ring(axis, step):
    count = lax.axis_size(axis)
    return lax.rem(lax.axis_index(axis) + (step + count), count)


def push(source, target, sems, index, axis, step):
    send, recv = sems
    copy = pltpu.make_async_remote_copy(
        src_ref=source,
        dst_ref=target,
        send_sem=send.at[index],
        recv_sem=recv.at[index],
        device_id={axis: ring(axis, step)},
        device_id_type=pl.DeviceIdType.MESH,
    )
    copy.start()
    return copy


def greet(peers):
    barrier = pltpu.get_barrier_semaphore()
    for axis, step in peers:
        pl.semaphore_signal(
            barrier,
            inc=1,
            device_id={axis: ring(axis, step)},
            device_id_type=pl.DeviceIdType.MESH,
        )
    pl.semaphore_wait(barrier, len(peers))


def halo_kernel(
    state_ref,
    cot_ref,
    sea_ref,
    home_ref,
    list_ref,
    flags_ref,
    state_edge_ref,
    cot_edge_ref,
    sea_edge_ref,
    state_rows_ref,
    cot_rows_ref,
    sea_rows_ref,
    lists,
    list_mine,
    edge_out,
    edge_in,
    rows_out,
    rows_in,
    list_send,
    list_recv,
    halo_send,
    halo_recv,
):
    rows, subs, width = state_ref.shape
    span = rows * subs
    lon_count = lax.axis_size("lon")
    cap = rows // lon_count
    lat_index = lax.axis_index("lat")
    peers = [("lon", d) for d in range(1, lon_count)] + [("lat", 1), ("lat", -1)]
    greet(peers)
    list_mine[...] = jnp.broadcast_to(list_ref[...], list_mine.shape)
    copies = []
    for d in range(1, lon_count):
        copies.append(push(list_mine, lists.at[d], (list_send, list_recv), d, "lon", d))
    for side, row in ((0, 0), (1, rows - 1)):
        rows_out[side, 0:subs] = state_ref[row]
        rows_out[side, subs : 2 * subs] = cot_ref[row]
        rows_out[side, 2 * subs : 2 * subs + 8] = jnp.broadcast_to(
            sea_ref[row : row + 1].astype(F32), (8, width)
        )
    halo = (halo_send, halo_recv)
    copies.append(push(rows_out.at[0], rows_in.at[1], halo, 0, "lat", -1))
    copies.append(push(rows_out.at[1], rows_in.at[0], halo, 1, "lat", 1))
    edge_out[:, 0:span] = pack_edges(state_ref[...].reshape(span, width))
    edge_out[:, span : 2 * span] = pack_edges(cot_ref[...].reshape(span, width))
    edge_out[:, 2 * span :] = pack_edges(sea_ref[...].astype(F32))
    copies.append(push(edge_out, edge_in.at[1], halo, 2, "lon", -1))
    copies.append(push(edge_out, edge_in.at[0], halo, 3, "lon", 1))
    for copy in copies:
        copy.wait()

    me = lax.axis_index("lon")
    home = home_ref[...]
    found = jnp.zeros(list_mine.shape, jnp.int32)
    for d in range(lon_count):
        entries = list_mine[...] if d == 0 else lists[d]
        owner = ring("lon", -d)
        source = entries // cap
        wanted = owner * cap + (entries - source * cap)
        hit = (source == me) & (wanted == home)
        found = jnp.where(hit, 1, found)
    flags_ref[...] = jnp.max(found, axis=0, keepdims=True)
    edges = between(edge_in[0], edge_in[1])
    state_edge_ref[...] = edges[:, 0:span]
    cot_edge_ref[...] = edges[:, span : 2 * span]
    sea_edge_ref[...] = edges[:, 2 * span :]
    inside = (lat_index > 0, lat_index < lax.axis_size("lat") - 1)
    state_rows_ref[...] = rows_in[:, 0:subs]
    cot_rows_ref[...] = rows_in[:, subs : 2 * subs]
    for side in range(2):
        open_here = jnp.where(inside[side], 1.0, 0.0)
        sea_rows_ref[side : side + 1] = rows_in[side, 2 * subs : 2 * subs + 1] * open_here
    sea_rows_ref[2:8] = jnp.zeros((6, width), F32)


def west_of(values, edge):
    rolled = pltpu.roll(values, 1, values.ndim - 1)
    return jnp.where(lane_of(values.shape) == 0, edge, rolled)


def east_of(values, edge):
    width = values.shape[-1]
    rolled = pltpu.roll(values, width - 1, values.ndim - 1)
    return jnp.where(lane_of(values.shape) == width - 1, edge, rolled)


def field_sum(values):
    values = values + pltpu.roll(values, 2, 1)
    return values + pltpu.roll(values, 4, 1)


def repeat_field(values, field):
    sub = lax.broadcasted_iota(jnp.int32, values.shape, 1)
    picked = jnp.where(sub // 2 == field, values, 0.0)
    return field_sum(picked)


def padded_load(ref, edges, start, size, total, offset):
    middle = ref[pl.ds(start, size)]
    if offset < 0:
        below = ref[pl.ds(jnp.maximum(start - 1, 0), 1)]
        below = jnp.where(start == 0, edges[0:1], below)
        return jnp.concatenate([below, middle[:-1]], axis=0)
    above = ref[pl.ds(jnp.minimum(start + size, total - 1), 1)]
    above = jnp.where(start + size >= total, edges[1:2], above)
    return jnp.concatenate([middle[1:], above], axis=0)


def prepare_sea(sea_ref, sea_edge_ref, sea_rows_ref, open_refs):
    rows, width = sea_ref.shape
    sea = sea_ref[...].astype(F32)
    edge = spread_edges(sea_edge_ref[...], width)
    south = jnp.concatenate([sea_rows_ref[0:1], sea[:-1]], axis=0)
    north = jnp.concatenate([sea[1:], sea_rows_ref[1:2]], axis=0)
    for ref, other in zip(open_refs, (west_of(sea, edge), east_of(sea, edge), south, north)):
        ref[...] = sea * other


def closure_kernel(
    flags_ref,
    features_ref,
    state_ref,
    cot_ref,
    sea_ref,
    state_edge_ref,
    cot_edge_ref,
    sea_edge_ref,
    state_rows_ref,
    cot_rows_ref,
    sea_rows_ref,
    w_in_ref,
    w_mid_ref,
    bias_in_ref,
    w_out_ref,
    bias_out_ref,
    diff_ref,
    diff_edge_ref,
    sums_ref,
    open_w,
    open_e,
    open_s,
    open_n,
    state_x,
    cot_x,
    kgrad,
    w_in_t,
    w_mid_t,
    bias_in_col,
    w_out_rep,
    w_out_col,
    bias_out_rep,
    acc_in,
    acc_mid,
    acc_out,
    acc_bias,
    acc_bout,
    order,
):
    rows, subs, width = state_ref.shape
    hid = w_mid_ref.shape[0]

    def note(row, count):
        order[count] = row
        return count + flags_ref[row]

    count = lax.fori_loop(0, rows, note, jnp.int32(0))
    for extra in range(GROUP):
        order[count + extra] = rows

    prepare_sea(sea_ref, sea_edge_ref, sea_rows_ref, (open_w, open_e, open_s, open_n))
    state_x[...] = spread_edges(state_edge_ref[...], width).reshape(rows, subs, width)
    cot_x[...] = spread_edges(cot_edge_ref[...], width).reshape(rows, subs, width)

    def kappa_chunk(step, carry):
        start = pl.multiple_of(step * CHUNK, CHUNK)
        at = pl.ds(start, CHUNK)
        q = state_ref[at]
        g = cot_ref[at]
        qx = state_x[at]
        gx = cot_x[at]

        def part(opened, q_near, g_near):
            return (g_near - g) * (q_near - q) * opened[at][:, None, :]

        total = part(open_w, west_of(q, qx), west_of(g, gx))
        total += part(open_e, east_of(q, qx), east_of(g, gx))
        total += part(
            open_s,
            padded_load(state_ref, state_rows_ref, start, CHUNK, rows, -1),
            padded_load(cot_ref, cot_rows_ref, start, CHUNK, rows, -1),
        )
        total += part(
            open_n,
            padded_load(state_ref, state_rows_ref, start, CHUNK, rows, 1),
            padded_load(cot_ref, cot_rows_ref, start, CHUNK, rows, 1),
        )
        kgrad[at] = field_sum(total) * -0.5
        diff_ref[at] = jnp.zeros((CHUNK, subs, width), F32)
        return carry

    lax.fori_loop(0, rows // CHUNK, kappa_chunk, 0)
    kgrad[pl.ds(rows, 8)] = jnp.zeros((8, subs, width), F32)

    levels = w_out_ref.shape[1]
    bias_in_col[...] = jnp.broadcast_to(bias_in_ref[...], (width, hid)).T
    w_out = w_out_ref[...]
    sub = lax.broadcasted_iota(jnp.int32, (8, levels), 0)
    lev = lax.broadcasted_iota(jnp.int32, (8, levels), 1)
    repeat = (lax.rem(sub, levels) == lev).astype(F32).astype(BF16)
    single = (sub == lev).astype(F32).astype(BF16)
    w_out_rep[...] = lax.dot_general(repeat, w_out, NT, preferred_element_type=F32).astype(BF16)
    w_out_col[...] = lax.dot_general(w_out, single, NT, preferred_element_type=F32).astype(BF16)
    level = lax.rem(lax.broadcasted_iota(jnp.int32, (8, width), 0), levels)
    bias_out = jnp.zeros((8, width), F32)
    for index in range(levels):
        bias_out = jnp.where(level == index, bias_out_ref[index], bias_out)
    bias_out_rep[...] = bias_out
    w_in_t[...] = w_in_ref[...].astype(F32).T.astype(BF16)
    w_mid_t[...] = w_mid_ref[...].astype(F32).T.astype(BF16)
    for ref in (acc_in, acc_mid, acc_out, acc_bias, acc_bout):
        ref[...] = jnp.zeros(ref.shape, F32)

    def group(step, carry):
        picked = [order[step * GROUP + i] for i in range(GROUP)]
        loads = [jnp.minimum(row, rows - 1) for row in picked]
        x = jnp.concatenate([features_ref[row] for row in loads], axis=1)
        kap = jnp.concatenate([kgrad[row] for row in picked], axis=1)
        bias_in = jnp.concatenate([bias_in_col[...]] * GROUP, axis=1)
        first = jnp.dot(w_in_t[...], x, preferred_element_type=F32) + bias_in
        h0 = jnp.tanh(first).astype(BF16)
        h1 = jnp.tanh(jnp.dot(w_mid_t[...], h0, preferred_element_type=F32)).astype(BF16)
        logits = jnp.dot(w_out_rep[...], h1, preferred_element_type=F32)
        logits = logits + jnp.concatenate([bias_out_rep[...]] * GROUP, axis=1)
        squashed = 1.0 / (1.0 + jnp.exp(-logits))
        for i, row in enumerate(picked):
            diff_ref[row] = kappa_most * squashed[:, i * width : (i + 1) * width]
        kap_low = kap.astype(BF16).astype(F32)
        logit_grad = kap_low * (kappa_most * squashed * (1.0 - squashed))
        logit_low = logit_grad.astype(BF16)
        acc_out[...] += lax.dot_general(logit_low, h1, NT, preferred_element_type=F32)
        acc_bout[...] += functools.reduce(
            jnp.add, [logit_grad[:, i * width : (i + 1) * width] for i in range(GROUP)]
        )
        carried = jnp.dot(w_out_col[...], logit_low, preferred_element_type=F32)
        current = h1.astype(F32)
        layer_grad = (carried * (1.0 - current * current)).astype(BF16)
        acc_mid[...] += lax.dot_general(h0, layer_grad, NT, preferred_element_type=F32)
        carried = jnp.dot(w_mid_ref[...], layer_grad, preferred_element_type=F32)
        base = h0.astype(F32)
        first_grad = carried * (1.0 - base * base)
        acc_bias[...] += functools.reduce(
            jnp.add, [first_grad[:, i * width : (i + 1) * width] for i in range(GROUP)]
        )
        acc_in[...] += lax.dot_general(
            x, first_grad.astype(BF16), NT, preferred_element_type=F32
        )
        return carry

    lax.fori_loop(0, (count + GROUP - 1) // GROUP, group, 0)

    scaling = 1.0 / math.sqrt(rows * width)
    f_in = w_in_ref.shape[0]
    ones = jnp.ones((8, width), F32)
    row_bias = lax.dot_general(ones, acc_bias[...], NT, precision=EXACT, preferred_element_type=F32)
    tall = jnp.concatenate([acc_bout[...], jnp.zeros((hid - 8, width), F32)], axis=0)
    row_bout = lax.dot_general(ones, tall, NT, precision=EXACT, preferred_element_type=F32)
    which = lax.broadcasted_iota(jnp.int32, (8, hid), 0)
    misc = jnp.where(which < 2, acc_out[...], jnp.where(which == 2, row_bias, row_bout))
    misc = jnp.where(which < 4, misc, 0.0)
    diff_edge_ref[...] = pack_edges(diff_ref[0:rows].reshape(rows * subs, width))
    tiles = 0
    for block in (acc_mid[...], acc_in[...], misc):
        for half in range(hid // width):
            count = block.shape[0] // 8
            part = block[:, half * width : (half + 1) * width] * scaling
            sums_ref[tiles : tiles + count] = part.reshape(count, 8, width)
            tiles += count
    spare = sums_ref.shape[0] - tiles
    if spare:
        sums_ref[tiles : tiles + spare] = jnp.zeros((spare, 8, width), F32)


def stencil_kernel(
    state_ref,
    cot_ref,
    sea_ref,
    diff_ref,
    state_edge_ref,
    cot_edge_ref,
    sea_edge_ref,
    diff_edge_ref,
    state_rows_ref,
    cot_rows_ref,
    sea_rows_ref,
    sums_ref,
    new_ref,
    adj_ref,
    grad_in_ref,
    grad_bias_in_ref,
    grad_mid_ref,
    grad_out_ref,
    grad_bias_out_ref,
    open_w,
    open_e,
    open_s,
    open_n,
    state_x,
    cot_x,
    diff_x,
    diff_rows_ref,
    edge_in,
    from_lat,
    for_lon,
    from_lon,
    chunk_sum,
    gathered,
    full,
    halo_send,
    halo_recv,
    lat_send,
    lat_recv,
    lon_send,
    lon_recv,
):
    rows, subs, width = state_ref.shape
    lat_count, lon_count = sums_ref.shape[:2]
    lat_me = lax.axis_index("lat")
    lon_me = lax.axis_index("lon")
    lat_steps = range(1, lat_count)
    lon_steps = range(1, lon_count)
    greet([("lon", d) for d in lon_steps] + [("lat", d) for d in lat_steps])
    halo = (halo_send, halo_recv)
    halo_copies = [
        push(diff_ref.at[0], diff_rows_ref.at[1], halo, 0, "lat", -1),
        push(diff_ref.at[rows - 1], diff_rows_ref.at[0], halo, 1, "lat", 1),
        push(diff_edge_ref, edge_in.at[1], halo, 2, "lon", -1),
        push(diff_edge_ref, edge_in.at[0], halo, 3, "lon", 1),
    ]
    lat_sems = (lat_send, lat_recv)
    lon_sems = (lon_send, lon_recv)
    reduce_lat = [
        push(sums_ref.at[ring("lat", d)], from_lat.at[d], lat_sems, d, "lat", d) for d in lat_steps
    ]
    prepare_sea(sea_ref, sea_edge_ref, sea_rows_ref, (open_w, open_e, open_s, open_n))
    state_x[...] = spread_edges(state_edge_ref[...], width).reshape(rows, subs, width)
    cot_x[...] = spread_edges(cot_edge_ref[...], width).reshape(rows, subs, width)
    for copy in halo_copies:
        copy.wait()
    diff_x[...] = spread_edges(between(edge_in[0], edge_in[1]), width).reshape(rows, subs, width)

    def chunk(step, carry):
        start = pl.multiple_of(step * CHUNK, CHUNK)
        at = pl.ds(start, CHUNK)
        q = state_ref[at]
        g = cot_ref[at]
        k = diff_ref[at]
        sub = lax.broadcasted_iota(jnp.int32, q.shape, 1)

        def face(sign, field, opened, q_near, g_near, k_near):
            gate = opened[at][:, None, :]
            speed = repeat_field(q + q_near, field) * (0.5 * gate)
            kf = (k + k_near) * (0.5 * gate)
            q_sum = 0.5 * (q + q_near)
            g_diff = g_near - g
            new_part = kf * (q_near - q) - sign * speed * q_sum
            w_part = field_sum(g_diff * q_sum) * ((0.5 * sign) * gate)
            adj_part = g_diff * (kf + (0.5 * sign) * speed)
            adj_part = adj_part + jnp.where(sub // 2 == field, w_part, 0.0)
            return new_part, adj_part

        qx, gx, kx = state_x[at], cot_x[at], diff_x[at]
        parts = [
            face(-1.0, 2, open_w, west_of(q, qx), west_of(g, gx), west_of(k, kx)),
            face(1.0, 2, open_e, east_of(q, qx), east_of(g, gx), east_of(k, kx)),
        ]
        for sign, offset, opened in ((-1.0, -1, open_s), (1.0, 1, open_n)):
            parts.append(
                face(
                    sign,
                    3,
                    opened,
                    padded_load(state_ref, state_rows_ref, start, CHUNK, rows, offset),
                    padded_load(cot_ref, cot_rows_ref, start, CHUNK, rows, offset),
                    padded_load(diff_ref, diff_rows_ref, start, CHUNK, rows, offset),
                )
            )
        new_ref[at] = q + parts[0][0] + parts[1][0] + parts[2][0] + parts[3][0]
        adj_ref[at] = g + parts[0][1] + parts[1][1] + parts[2][1] + parts[3][1]
        return carry

    steps = rows // CHUNK
    quarter = steps // 4
    lax.fori_loop(0, quarter, chunk, 0)
    for copy in reduce_lat:
        copy.wait()
    total = sums_ref[lat_me]
    for d in lat_steps:
        total = total + from_lat[d]
    for_lon[...] = total
    reduce_lon = [
        push(for_lon.at[ring("lon", d)], from_lon.at[d], lon_sems, d, "lon", d) for d in lon_steps
    ]
    lax.fori_loop(quarter, 2 * quarter, chunk, 0)
    for copy in reduce_lon:
        copy.wait()
    total = for_lon[lon_me]
    for d in lon_steps:
        total = total + from_lon[d]
    chunk_sum[...] = total
    gathered[lon_me] = total
    spread_lon = [
        push(chunk_sum, gathered.at[lon_me], lon_sems, lon_count + d, "lon", d) for d in lon_steps
    ]
    lax.fori_loop(2 * quarter, 3 * quarter, chunk, 0)
    for copy in spread_lon:
        copy.wait()
    spread_lat = [
        push(gathered, full.at[lat_me], lat_sems, lat_count + d, "lat", d) for d in lat_steps
    ]
    full[lat_me] = gathered[...]
    lax.fori_loop(3 * quarter, steps, chunk, 0)
    for copy in spread_lat:
        copy.wait()

    hid = grad_mid_ref.shape[0]
    flat = full[...].reshape(lat_count * lon_count * full.shape[2], 8, width)
    tiles = 0
    halves = hid // width
    for ref in (grad_mid_ref, grad_in_ref):
        count = ref.shape[0] // 8
        for half in range(halves):
            ref[:, half * width : (half + 1) * width] = flat[tiles : tiles + count].reshape(
                8 * count, width
            )
            tiles += count
    misc = jnp.concatenate([flat[tiles + half] for half in range(halves)], axis=1)
    levels = grad_out_ref.shape[1]
    grad_bias_in_ref[...] = misc[2:3]
    grad_bias_out_ref[...] = misc[3:4, 0:levels]
    grad_out_ref[...] = misc.T[:, 0:levels]


def on_device(
    ocean_state,
    cotangent,
    features,
    w_in,
    bias_in,
    w_mid,
    w_out,
    bias_out,
    land_mask,
    home_slot,
    owner_list,
):
    rows, fields, levels, width = ocean_state.shape
    subs = fields * levels
    f_in, hid = w_in.shape
    lon_count = lax.axis_size("lon")
    lat_count = lax.axis_size("lat")

    state = ocean_state.reshape(rows, subs, width)
    cot = cotangent.reshape(rows, subs, width)
    sea = land_mask
    span = rows * subs
    vmem = pl.BlockSpec(memory_space=pltpu.VMEM)
    smem = pl.BlockSpec(memory_space=pltpu.SMEM)
    dma = pltpu.SemaphoreType.DMA
    listed = owner_list.shape[0]
    flags, state_edge, cot_edge, sea_edge, state_rows, cot_rows, sea_rows = pl.pallas_call(
        halo_kernel,
        name="halo",
        out_shape=(
            jax.ShapeDtypeStruct((1, rows), jnp.int32),
            jax.ShapeDtypeStruct((8, span), F32),
            jax.ShapeDtypeStruct((8, span), F32),
            jax.ShapeDtypeStruct((8, rows), F32),
            jax.ShapeDtypeStruct((2, subs, width), F32),
            jax.ShapeDtypeStruct((2, subs, width), F32),
            jax.ShapeDtypeStruct((8, width), F32),
        ),
        in_specs=[vmem] * 5,
        out_specs=(vmem,) * 7,
        scratch_shapes=[
            pltpu.VMEM((lon_count, listed, rows), jnp.int32),
            pltpu.VMEM((listed, rows), jnp.int32),
            pltpu.VMEM((8, 2 * span + rows), F32),
            pltpu.VMEM((2, 8, 2 * span + rows), F32),
            pltpu.VMEM((2, 2 * subs + 8, width), F32),
            pltpu.VMEM((2, 2 * subs + 8, width), F32),
            dma((lon_count,)),
            dma((lon_count,)),
            dma((4,)),
            dma((4,)),
        ],
        compiler_params=pltpu.CompilerParams(
            collective_id=0, has_side_effects=True, vmem_limit_bytes=32 * 1024 * 1024
        ),
    )(
        state,
        cot,
        sea,
        home_slot.reshape(1, rows),
        owner_list,
    )
    flags = flags.reshape(rows)

    tiles = (hid // width) * (hid + f_in + 8) // 8
    share = -(-tiles // (lat_count * lon_count))
    mask = pltpu.VMEM((rows, width), F32)
    slab = pltpu.VMEM((rows, subs, width), F32)
    diff, diff_edge, sums = pl.pallas_call(
        closure_kernel,
        name="closure",
        out_shape=(
            jax.ShapeDtypeStruct((rows + 8, subs, width), F32),
            jax.ShapeDtypeStruct((8, span), F32),
            jax.ShapeDtypeStruct((lat_count * lon_count * share, 8, width), F32),
        ),
        in_specs=[smem] + [vmem] * 14 + [smem],
        out_specs=(vmem,) * 3,
        scratch_shapes=[
            mask,
            mask,
            mask,
            mask,
            slab,
            slab,
            pltpu.VMEM((rows + 8, subs, width), F32),
            pltpu.VMEM((hid, f_in), BF16),
            pltpu.VMEM((hid, hid), BF16),
            pltpu.VMEM((hid, width), F32),
            pltpu.VMEM((8, hid), BF16),
            pltpu.VMEM((hid, 8), BF16),
            pltpu.VMEM((8, width), F32),
            pltpu.VMEM((f_in, hid), F32),
            pltpu.VMEM((hid, hid), F32),
            pltpu.VMEM((8, hid), F32),
            pltpu.VMEM((hid, width), F32),
            pltpu.VMEM((8, width), F32),
            pltpu.SMEM((rows + 2 * GROUP,), jnp.int32),
        ],
        compiler_params=pltpu.CompilerParams(vmem_limit_bytes=40 * 1024 * 1024),
    )(
        flags,
        features,
        state,
        cot,
        sea,
        state_edge,
        cot_edge,
        sea_edge,
        state_rows,
        cot_rows,
        sea_rows,
        w_in,
        w_mid[0],
        bias_in[None],
        w_out,
        bias_out,
    )

    piece = (share, 8, width)
    new_state, adjoint, grad_in, grad_bias_in, grad_mid, grad_out, grad_bias_out = pl.pallas_call(
        stencil_kernel,
        name="stencil",
        out_shape=(
            jax.ShapeDtypeStruct((rows, subs, width), F32),
            jax.ShapeDtypeStruct((rows, subs, width), F32),
            jax.ShapeDtypeStruct((f_in, hid), F32),
            jax.ShapeDtypeStruct((1, hid), F32),
            jax.ShapeDtypeStruct((hid, hid), F32),
            jax.ShapeDtypeStruct((hid, levels), F32),
            jax.ShapeDtypeStruct((1, levels), F32),
        ),
        in_specs=[vmem] * 12,
        out_specs=(vmem,) * 7,
        scratch_shapes=[
            mask,
            mask,
            mask,
            mask,
            slab,
            slab,
            slab,
            pltpu.VMEM((2, subs, width), F32),
            pltpu.VMEM((2, 8, span), F32),
            pltpu.VMEM((lat_count, lon_count) + piece, F32),
            pltpu.VMEM((lon_count,) + piece, F32),
            pltpu.VMEM((lon_count,) + piece, F32),
            pltpu.VMEM(piece, F32),
            pltpu.VMEM((lon_count,) + piece, F32),
            pltpu.VMEM((lat_count, lon_count) + piece, F32),
            dma((4,)),
            dma((4,)),
            dma((2 * lat_count,)),
            dma((2 * lat_count,)),
            dma((2 * lon_count,)),
            dma((2 * lon_count,)),
        ],
        compiler_params=pltpu.CompilerParams(
            collective_id=1, has_side_effects=True, vmem_limit_bytes=32 * 1024 * 1024
        ),
    )(
        state,
        cot,
        sea,
        diff,
        state_edge,
        cot_edge,
        sea_edge,
        diff_edge,
        state_rows,
        cot_rows,
        sea_rows,
        sums.reshape((lat_count, lon_count) + piece),
    )
    return (
        new_state.reshape(ocean_state.shape),
        adjoint.reshape(ocean_state.shape),
        grad_in,
        grad_bias_in[0],
        grad_mid[None],
        grad_out,
        grad_bias_out[0],
    )


def solution(mesh):
    in_specs = (
        P("lat", None, None, "lon"),
        P("lat", None, None, "lon"),
        P("lat", None, "lon"),
        P(),
        P(),
        P(),
        P(),
        P(),
        P("lat", "lon"),
        P("lat", "lon"),
        P("lat", "lon"),
    )
    out_specs = (P("lat", None, None, "lon"), P("lat", None, None, "lon"), P(), P(), P(), P(), P())
    return jax.shard_map(
        on_device, mesh=mesh, in_specs=in_specs, out_specs=out_specs, check_vma=False
    )
```
